32 devices in a mesh: grp: 4 (over y, core), leaf: 8 (over z, x).
Axes of the slice: x: 2, y: 2, z: 4, core: 2. Of those that a mesh axis runs over, the one named last changes fastest.
Arguments:
- points: bfloat16 [131072, 64], P(('grp', 'leaf')), may hold values from -6 to 6
- solution: float32 [131072, 64], P(('grp', 'leaf')), may hold values from -6 to 6
- residual: float32 [131072, 64], P(('grp', 'leaf')), may hold values from -150 to 150
- direction: float32 [131072, 64], P(('grp', 'leaf')), may hold values from -150 to 150
- near: int32 [128, 3], P(('grp', 'leaf')), may hold values from -1 to 127, as said below
- bases: bfloat16 [128, 1024, 256], P(('grp', 'leaf')), may hold values from -0.1875 to 0.1875
- leaf_transfer: bfloat16 [128, 256, 256], P(('grp', 'leaf')), may hold values from -0.1875 to 0.1875
- inner_transfer: bfloat16 [3, 2, 256, 256], replicated, may hold values from -1 to 1
- inner_coupling: bfloat16 [3, 256, 256], replicated, may hold values from -1 to 1
- outer_transfer: bfloat16 [2, 2, 256, 256], replicated, may hold values from -1 to 1
- outer_coupling: bfloat16 [2, 256, 256], replicated, may hold values from -1 to 1
Outputs:
- new_solution: float32 [131072, 64], P(('grp', 'leaf'))
- new_residual: float32 [131072, 64], P(('grp', 'leaf'))
- new_direction: float32 [131072, 64], P(('grp', 'leaf'))
The draws below stay inside these ranges and needn't reach their ends.
Inputs may be any that keep to these rules, and one draw needn't show every extreme that they name: Row i of near is (i, i - 1 or -1, i + 1 or -1); leaf i lists i + 1 exactly when leaf i + 1 lists i; the last leaf of each aligned block of 4 leaves lists the next leaf whenever there is one.
All inputs are finite; a program needn't handle non-finite values.
Results may differ from the reference program's by a relative error of at most 0.0027.
Values may be sent and summed in bfloat16 or wider, within the bound.
A program may use at most 128 MiB of HBM per device.

```python
import jax
import jax.numpy as jnp
from jax import lax

DIM = 64
LEAF = 1024
RANK = 256
NRHS = 64
LEAF_DEV = 4
LEAVES = 128
POINTS = 131072
LEVELS_LEAF = 3
LEVELS_GRP = 2
DEVICES = 32


def scaled_rows(key):
    first, second, third = jax.random.split(key, 3)
    where_row = jnp.arange(POINTS, dtype=jnp.float32) / POINTS
    col_scale = jnp.exp(jax.random.uniform(third, (NRHS,), jnp.float32) * jnp.log(10.0)) / jnp.sqrt(10.0)
    row_spread = jnp.exp(jax.random.uniform(second, (POINTS,), jnp.float32) * jnp.log(10.0))
    base = jnp.clip(jax.random.normal(first, (POINTS, NRHS), jnp.float32), -6.0, 6.0)
    row_scale = (1.0 + 2.0 * where_row) * row_spread / 4.0
    return base * row_scale[:, None] * col_scale[None, :]


def draw_residual(key, part):
    return scaled_rows(jax.random.fold_in(key, 101))


def draw_direction(key, part):
    return scaled_rows(jax.random.fold_in(key, 202))


def draw_near(key, part):
    links = jax.random.randint(jax.random.fold_in(key, 303), (LEAVES - 1,), 0, 4) > 0
    index = jnp.arange(LEAVES, dtype=jnp.int32)
    forced = (index[:-1] + 1) % LEAF_DEV == 0
    links = jnp.logical_or(links, forced)
    has_left = jnp.concatenate([jnp.zeros((1,), bool), links])
    has_right = jnp.concatenate([links, jnp.zeros((1,), bool)])
    left = jnp.where(has_left, index - 1, -1)
    right = jnp.where(has_right, index + 1, -1)
    return jnp.stack([index, left, right], axis=1).astype(jnp.int32)


def signed_table(key, shape, spread, clip_at):
    return jnp.clip(jax.random.normal(key, shape, jnp.float32), -clip_at, clip_at) * spread


def transfer_spread():
    return (70.0 / (99.0 * RANK)) ** 0.5


def coupling_spread():
    return 0.5 / RANK ** 0.5


def draw_bases(key, part):
    return signed_table(jax.random.fold_in(key, 808), (LEAVES, LEAF, RANK), LEAF ** (-0.5), 6.0).astype(jnp.bfloat16)


def draw_leaf_transfer(key, part):
    return signed_table(jax.random.fold_in(key, 909), (LEAVES, RANK, RANK), (LEAF_DEV * RANK) ** (-0.5), 6.0).astype(jnp.bfloat16)


def draw_inner_transfer(key, part):
    return signed_table(jax.random.fold_in(key, 404), (LEVELS_LEAF, 2, RANK, RANK), transfer_spread(), 4.0).astype(jnp.bfloat16)


def draw_outer_transfer(key, part):
    return signed_table(jax.random.fold_in(key, 505), (LEVELS_GRP, 2, RANK, RANK), transfer_spread(), 4.0).astype(jnp.bfloat16)


def draw_inner_coupling(key, part):
    return signed_table(jax.random.fold_in(key, 606), (LEVELS_LEAF, RANK, RANK), coupling_spread(), 4.0).astype(jnp.bfloat16)


def draw_outer_coupling(key, part):
    return signed_table(jax.random.fold_in(key, 707), (LEVELS_GRP, RANK, RANK), coupling_spread(), 4.0).astype(jnp.bfloat16)


def block_levels(rng, extent, cuts, low, top_value):
    def one(position, parts):
        draws = jax.random.uniform(jax.random.fold_in(jax.random.fold_in(rng, 6), position), (parts,), jnp.float32, low / len(cuts), top_value / len(cuts))
        return jnp.repeat(jnp.exp(draws), extent[position] // parts).reshape((-1,) + (1,) * (len(extent) - position - 1))

    loudness = one(*cuts[0])
    for cut in cuts[1:]:
        loudness = loudness * one(*cut)
    return loudness


def noise(key, extent, scale, reach, cuts=(), kind=jnp.bfloat16):
    drawn = scale * jax.random.normal(key, extent, jnp.float32)
    if cuts:
        drawn = drawn * block_levels(key, extent, cuts, -0.22, 0.18)
    return jnp.clip(drawn, -reach, reach).astype(kind)


def setup_inputs(seed: int = 0) -> dict:
    streams_of = jax.random.split(jax.random.key(seed), 12)
    return {
        "points": noise(streams_of[0], (POINTS, DIM), 1.0, 6.0, ((0, 32),)),
        "solution": noise(streams_of[1], (POINTS, NRHS), 1.0, 6.0, ((0, 32),), jnp.float32),
        "residual": draw_residual(jax.random.fold_in(streams_of[11], 71), 0),
        "direction": draw_direction(jax.random.fold_in(streams_of[11], 71), 0),
        "near": draw_near(jax.random.fold_in(streams_of[11], 71), 0),
        "bases": draw_bases(jax.random.fold_in(streams_of[11], 71), 0),
        "leaf_transfer": draw_leaf_transfer(jax.random.fold_in(streams_of[11], 71), 0),
        "inner_transfer": draw_inner_transfer(jax.random.fold_in(streams_of[11], 71), 0),
        "inner_coupling": draw_inner_coupling(jax.random.fold_in(streams_of[11], 71), 0),
        "outer_transfer": draw_outer_transfer(jax.random.fold_in(streams_of[11], 71), 0),
        "outer_coupling": draw_outer_coupling(jax.random.fold_in(streams_of[11], 71), 0),
    }


highest = lax.Precision.HIGHEST
ridge = 2.0


def kernel_block(own, window, mask):
    own_wide = own.astype(jnp.float32)
    win_wide = window.astype(jnp.float32)
    sq_own = jnp.sum(own_wide * own_wide, axis=1)
    sq_win = jnp.sum(win_wide * win_wide, axis=1)
    cross = jnp.dot(own, window.T, preferred_element_type=jnp.float32)
    dist = sq_own[:, None] + sq_win[None, :] - 2.0 * cross
    return (jnp.exp(-dist * (2.0 / own.shape[1])) * mask[None, :]).astype(jnp.bfloat16)


def near_field(points, packed, near):
    def one(index):
        ids = near[index]
        order = [ids[1], ids[0], ids[2]]
        pts_list = []
        vec_list = []
        mask_list = []
        for ident in order:
            start = (jnp.clip(ident, 0, LEAVES - 1) * LEAF).astype(jnp.int32)
            pts_list.append(lax.dynamic_slice_in_dim(points, start, LEAF, 0))
            vec_list.append(lax.dynamic_slice_in_dim(packed, start, LEAF, 0))
            mask_list.append(jnp.where(ident >= 0, 1.0, 0.0).astype(jnp.float32) * jnp.ones((LEAF,), jnp.float32))
        own = lax.dynamic_slice_in_dim(points, (index * LEAF).astype(jnp.int32), LEAF, 0)
        kern = kernel_block(own, jnp.concatenate(pts_list, 0), jnp.concatenate(mask_list, 0))
        return jnp.dot(kern, jnp.concatenate(vec_list, 0), preferred_element_type=jnp.float32)

    result = lax.map(one, jnp.arange(LEAVES, dtype=jnp.int32))
    return result.reshape(POINTS, NRHS)


def far_field(packed, bases, leaf_transfer, inner_transfer, inner_coupling, outer_transfer, outer_coupling):
    vectors = packed.reshape(LEAVES, LEAF, NRHS).astype(jnp.float32)
    skel = jnp.einsum('lpr,lpc->lrc', bases.astype(jnp.float32), vectors, precision=highest)
    trans = leaf_transfer.astype(jnp.float32).reshape(DEVICES, LEAF_DEV, RANK, RANK)
    nodes = jnp.einsum('dlba,dlbc->dac', trans, skel.reshape(DEVICES, LEAF_DEV, RANK, NRHS), precision=highest)
    q_all = jnp.concatenate([inner_transfer, outer_transfer], 0).astype(jnp.float32)
    b_all = jnp.concatenate([inner_coupling, outer_coupling], 0).astype(jnp.float32)
    couplings = []
    for level in range(q_all.shape[0]):
        left = nodes[0::2]
        right = nodes[1::2]
        to_left = jnp.einsum('ab,nbc->nac', b_all[level], right, precision=highest)
        to_right = jnp.einsum('ba,nbc->nac', b_all[level], left, precision=highest)
        couplings.append((to_left, to_right))
        nodes = jnp.einsum('ba,nbc->nac', q_all[level, 0], left, precision=highest) + jnp.einsum('ba,nbc->nac', q_all[level, 1], right, precision=highest)
    incoming = jnp.zeros((1, RANK, NRHS), jnp.float32)
    for level in reversed(range(q_all.shape[0])):
        to_left, to_right = couplings[level]
        left_in = to_left + jnp.einsum('ab,nbc->nac', q_all[level, 0], incoming, precision=highest)
        right_in = to_right + jnp.einsum('ab,nbc->nac', q_all[level, 1], incoming, precision=highest)
        incoming = jnp.stack([left_in, right_in], 1).reshape(-1, RANK, NRHS)
    leaf_in = jnp.einsum('dlab,dbc->dlac', trans, incoming, precision=highest).reshape(LEAVES, RANK, NRHS).astype(jnp.bfloat16)
    result = jnp.einsum('lpr,lrc->lpc', bases.astype(jnp.float32), leaf_in.astype(jnp.float32), precision=highest)
    return result.reshape(POINTS, NRHS)


def reference(points, solution, residual, direction, near, bases, leaf_transfer, inner_transfer, inner_coupling, outer_transfer, outer_coupling):
    packed = direction.astype(jnp.bfloat16)
    near_term = near_field(points, packed, near)
    far_term = far_field(packed, bases, leaf_transfer, inner_transfer, inner_coupling, outer_transfer, outer_coupling)
    image = ridge * direction + near_term + far_term
    rr = jnp.sum(residual * residual, axis=0)
    pq = jnp.sum(direction * image, axis=0)
    alpha = rr / pq
    new_solution = solution + alpha * direction
    new_residual = residual - alpha * image
    fresh = jnp.sum(new_residual * new_residual, axis=0)
    new_direction = new_residual + (fresh / rr) * direction
    return new_solution, new_residual, new_direction
```

```python
import functools
import math

import jax
import jax.numpy as jnp
from jax import lax
from jax.experimental import pallas as pl
from jax.experimental.pallas import tpu as pltpu
from jax.sharding import PartitionSpec as P

MESH = pl.DeviceIdType.MESH
ridge = 2.0
f32 = jnp.float32
bf16 = jnp.bfloat16
vmem = pl.BlockSpec(memory_space=pltpu.VMEM)
smem = pl.BlockSpec(memory_space=pltpu.SMEM)


def nn(a, b):
    return jnp.dot(a, b, preferred_element_type=f32)


def nt(a, b):
    return lax.dot_general(a, b, (((1,), (1,)), ((), ())), preferred_element_type=f32)


def split(value):
    high = value.astype(bf16)
    low = (value - high.astype(f32)).astype(bf16)
    return jnp.concatenate([high, low], axis=0)


def fold(stacked):
    half = stacked.shape[0] // 2
    return stacked[:half] + stacked[half:]


TILE = 512
HALO_AT = 1
JOBS = ((3,), (3, 1))
PARTS = 4


def step_kernel(
    groups, leaves, near_hbm, inner_q_hbm, inner_b_hbm, outer_q_hbm, outer_b_hbm,
    points_hbm, trans_hbm, bases_hbm, direction_hbm, residual_hbm, solution_hbm,
    image_ref, sums_ref, direction_ref, residual_ref, solution_ref,
    near_ref, inner_q, inner_b, outer_q, outer_b, joint_ref, node_ref, halo_ref, source, target, trans_ref, bases_ref, totals,
    node_send, node_recv, halo_send, halo_recv, total_send, total_recv, load_sem,
):
    leaf_dev, leaf = bases_ref.shape[:2]
    nrhs = image_ref.shape[0]
    dim = joint_ref.shape[0] - nrhs
    inner = inner_q.shape[0]
    outer = outer_q.shape[0]
    depth = inner + outer

    pairs = {}
    for i in range(leaf_dev):
        cols = pl.ds(i * leaf, leaf)
        pairs["direction", i] = (direction_hbm.at[:, cols], direction_ref.at[:, cols])
        pairs["bases", i] = (bases_hbm.at[i], bases_ref.at[i])
    pairs["trans"] = (trans_hbm, trans_ref)
    pairs["points"] = (points_hbm, joint_ref.at[pl.ds(0, dim), :])
    pairs["near"] = (near_hbm, near_ref)
    pairs["iq"] = (inner_q_hbm, inner_q)
    pairs["ib"] = (inner_b_hbm, inner_b)
    pairs["oq"] = (outer_q_hbm, outer_q)
    pairs["ob"] = (outer_b_hbm, outer_b)
    pairs["residual"] = (residual_hbm, residual_ref)
    pairs["solution"] = (solution_hbm, solution_ref)
    loads = {key: pltpu.make_async_copy(a, b, load_sem.at[n]) for n, (key, (a, b)) in enumerate(pairs.items())}
    for load in loads.values():
        load.start()

    grp = lax.axis_index("grp")
    pos = lax.axis_index("leaf")
    me = grp * leaves + pos
    count = groups * leaves
    right = lax.rem(me + 1, count)
    left = lax.rem(me + count - 1, count)
    right_id = (right // leaves, lax.rem(right, leaves))
    left_id = (left // leaves, lax.rem(left, leaves))
    bits = [lax.rem(pos // (1 << k), 2) for k in range(inner)]
    bits += [lax.rem(grp // (1 << k), 2) for k in range(outer)]

    def peer(flips):
        g, p = grp, pos
        for k in flips:
            if k < inner:
                p = p + (1 - 2 * bits[k]) * (1 << k)
            else:
                g = g + (1 - 2 * bits[k]) * (1 << (k - inner))
        return g, p

    def subset(slot, order):
        return tuple(k for n, k in enumerate(order) if slot >> n & 1)

    stages = tree_stages(inner, outer)
    sum_stages = total_stages(inner, outer)

    barrier = pltpu.get_barrier_semaphore()
    met = set()
    for steps in stages:
        met |= {subset(s, step) for step in steps for s in range(1, 1 << len(step))}
    for order in sum_stages:
        met |= {subset(s, order) for s in range(1, 1 << len(order))}
    met = {tuple(sorted(flips)) for flips in met}
    greeted = [peer(flips) for flips in sorted(met)]
    if len(met) < count - 1:
        greeted += [left_id, right_id]
    for who in greeted:
        pl.semaphore_signal(barrier, inc=1, device_id=who, device_id_type=MESH)

    last = joint_ref.shape[1] - leaf

    def halo(side, first_row, height):
        start, who = ((last, right_id), (0, left_id))[side]
        n = 2 * side + (1 if first_row else 0)
        rows = pl.ds(first_row, height)
        return pltpu.make_async_remote_copy(
            src_ref=joint_ref.at[rows, pl.ds(start, leaf)], dst_ref=halo_ref.at[side, rows, :],
            send_sem=halo_send.at[n], recv_sem=halo_recv.at[n], device_id=who, device_id_type=MESH,
        )

    halo_points = [halo(side, 0, dim) for side in range(2)]
    halo_values = [halo(side, dim, nrhs) for side in range(2)]

    node = None
    for i in range(leaf_dev):
        cols = slice(i * leaf, (i + 1) * leaf)
        loads["direction", i].wait()
        joint_ref[dim:, cols] = direction_ref[:, cols].astype(bf16)
        loads["bases", i].wait()
        skel = nn(joint_ref[dim:, cols], bases_ref[i])
        if i == 0:
            loads["trans"].wait()
        term = nn(split(skel), trans_ref[i])
        node = term if node is None else node + term
    node = fold(node)

    tile = min(leaf, TILE)
    scale = 2.0 / dim * math.log2(math.e)

    def parts(pts):
        wide = pts.astype(f32)
        sq = jnp.sum(wide * wide, axis=0, keepdims=True)
        high = sq.astype(bf16).astype(f32)
        mid = (sq - high).astype(bf16).astype(f32)
        low = sq - high - mid
        row = lax.broadcasted_iota(jnp.int32, (128 - dim, pts.shape[1]), 0)

        def extra(first, second):
            ones = jnp.where(jnp.logical_and(row >= second, row < second + 3), 1.0, 0.0)
            return jnp.where(row == first, -high, jnp.where(row == first + 1, -mid, jnp.where(row == first + 2, -low, ones)))

        return wide, extra

    def put_source(slot, wide, extra):
        source[slot] = jnp.concatenate([2.0 * wide, extra(0, 3)], axis=0).T.astype(bf16)

    def block(i, slot, values):
        acc = jnp.zeros((nrhs, leaf), f32)
        for t in range(leaf // tile):
            power = nn(source[slot, t * tile : (t + 1) * tile, :], target[i])
            kern = jnp.exp2(power * scale).astype(bf16)
            acc += nn(values(t), kern)
        return acc

    def own(j):
        return lambda t: joint_ref[dim:, j * leaf + t * tile : j * leaf + (t + 1) * tile]

    def edge(side):
        return lambda t: halo_ref[side, dim:, t * tile : (t + 1) * tile]

    def itself(i):
        cols = slice(i * leaf, (i + 1) * leaf)
        wide, extra = parts(joint_ref[:dim, cols])
        put_source(i + 1, wide, extra)
        target[i] = jnp.concatenate([wide, extra(3, 0)], axis=0).astype(bf16)
        image_ref[:, cols] = ridge * direction_ref[:, cols] + block(i, i + 1, own(i))

    def beside(i):
        here = jnp.where(near_ref[i, 2] >= 0, 1.0, 0.0).astype(f32)
        there = jnp.where(near_ref[i + 1, 1] >= 0, 1.0, 0.0).astype(f32)
        mine = joint_ref[dim:, i * leaf : (i + 1) * leaf]
        values = own(i + 1)
        acc = jnp.zeros((nrhs, leaf), f32)
        for t in range(leaf // tile):
            power = nn(source[i + 2, t * tile : (t + 1) * tile, :], target[i])
            kern = jnp.exp2(power * scale).astype(bf16)
            acc += nn(values(t), kern)
            cols = slice((i + 1) * leaf + t * tile, (i + 1) * leaf + (t + 1) * tile)
            image_ref[:, cols] += there * nt(mine, kern)
        image_ref[:, i * leaf : (i + 1) * leaf] += here * acc

    def outside(side):
        i, column, slot = ((0, 1, 0), (leaf_dev - 1, 2, leaf_dev + 1))[side]
        halo_points[side].wait()
        halo_values[side].wait()
        put_source(slot, *parts(halo_ref[side, :dim, :]))
        flag = jnp.where(near_ref[i, column] >= 0, 1.0, 0.0).astype(f32)
        image_ref[:, i * leaf : (i + 1) * leaf] += flag * block(i, slot, edge(side))

    jobs = [functools.partial(itself, i) for i in range(leaf_dev)]
    jobs += [functools.partial(beside, i) for i in range(leaf_dev - 1)]
    jobs += [functools.partial(outside, side) for side in range(2)]

    pl.semaphore_wait(barrier, len(greeted))
    loads["points"].wait()
    loads["near"].wait()
    if HALO_AT == 0:
        for copy in halo_points + halo_values:
            copy.start()

    def tables(k):
        return (inner_q, inner_b, k) if k < inner else (outer_q, outer_b, k - inner)

    def rows_of(pieces):
        return jnp.concatenate(pieces, axis=0) if len(pieces) > 1 else pieces[0]

    def product(groups_of_pieces, matrix, op):
        flat = [piece for pieces in groups_of_pieces for piece in pieces]
        out = op(rows_of(flat), matrix)
        sums, at = [], 0
        for pieces in groups_of_pieces:
            total = None
            for _ in pieces:
                part = out[at * nrhs : (at + 1) * nrhs]
                total = part if total is None else total + part
                at += 1
            sums.append(total)
        return sums

    def pair(value):
        high = value.astype(bf16)
        return [high, (value - high.astype(f32)).astype(bf16)]

    records = []
    sent = []
    for c, steps in enumerate(stages):
        order = [k for step in steps for k in step]
        node_ref[c, :nrhs] = node.astype(bf16)
        held = 1
        for n, step in enumerate(steps):
            copies = []
            for s in range(1, 1 << len(step)):
                copies.append(pltpu.make_async_remote_copy(
                    src_ref=node_ref.at[c, pl.ds(0, held * nrhs), :],
                    dst_ref=node_ref.at[c, pl.ds(s * held * nrhs, held * nrhs), :],
                    send_sem=node_send.at[c, s * held], recv_sem=node_recv.at[c, s * held],
                    device_id=peer(subset(s, step)), device_id_type=MESH,
                ))
            for copy in reversed(copies):
                copy.start()
            if (c, n) == (0, 0):
                if HALO_AT == 1:
                    for copy in halo_points + halo_values:
                        copy.start()
                for key in ("iq", "ib", "oq", "ob"):
                    loads[key].wait()
            take = JOBS[c][n] if c < len(JOBS) and n < len(JOBS[c]) else 0
            for job in jobs[:take]:
                job()
            jobs = jobs[take:]
            for copy in copies:
                copy.wait_recv()
            if (c, n) == (0, 0) and HALO_AT == 2:
                for copy in halo_points + halo_values:
                    copy.start()
            sent += copies
            held <<= len(step)
        if c == len(stages) - 1:
            for job in jobs:
                job()
        current = {s: [node_ref[c, s * nrhs : (s + 1) * nrhs]] for s in range(1, held)}
        current[0] = pair(node)
        final = c == len(stages) - 1
        for k in sorted(order):
            b = 1 << order.index(k)
            q_ref, b_ref, index = tables(k)
            mat = b_ref[index]
            sibling = [current[b]]
            records.append(jnp.where(bits[k] == 0, product(sibling, mat, nt)[0], product(sibling, mat, nn)[0]))
            low = [s for s in sorted(current) if not s & b and not (final and s == 0)]
            if low:
                mine = product([current[s] for s in low], q_ref[index, bits[k]], nn)
                other = product([current[s | b] for s in low], q_ref[index, 1 - bits[k]], nn)
                merged = {s: x + y for s, x, y in zip(low, mine, other)}
            else:
                merged = {}
            if not final:
                node = merged[0]
            current = {s: pair(v) for s, v in merged.items()}

    incoming = records[-1]
    for k in reversed(range(depth - 1)):
        q_ref, _, index = tables(k)
        incoming = records[k] + product([pair(incoming)], q_ref[index, bits[k]], nt)[0]

    def narrow(value):
        out = value[:, :128]
        for c in range(1, value.shape[1] // 128):
            out += value[:, c * 128 : (c + 1) * 128]
        return out

    stacked = split(incoming)
    loads["residual"].wait()
    loads["solution"].wait()
    inputs = [fold(nt(stacked, trans_ref[i])).astype(bf16) for i in range(leaf_dev)]
    sums = [jnp.zeros((nrhs, 128), f32)] * 4
    for i in range(leaf_dev):
        cols = slice(i * leaf, (i + 1) * leaf)
        image = image_ref[:, cols] + nt(inputs[i], bases_ref[i])
        image_ref[:, cols] = image
        way = direction_ref[:, cols]
        rest = residual_ref[:, cols]
        terms = (rest * rest, way * image, rest * image, image * image)
        sums = [s + narrow(t) for s, t in zip(sums, terms)]
    rows = [jnp.sum(s.T, axis=0, keepdims=True) for s in sums]
    total = jnp.concatenate(rows + [jnp.zeros((4, nrhs), f32)], axis=0)

    at = 0
    for order in sum_stages:
        slots = 1 << len(order)
        totals[at] = total
        copies = []
        for s in sorted(range(1, slots), key=lambda s: -sum(distance(k, inner) for k in subset(s, order))):
            copies.append(pltpu.make_async_remote_copy(
                src_ref=totals.at[at], dst_ref=totals.at[at + s],
                send_sem=total_send.at[at + s], recv_sem=total_recv.at[at + s],
                device_id=peer(subset(s, order)), device_id_type=MESH,
            ))
        for copy in copies:
            copy.start()
        sent += copies
        for copy in reversed(copies):
            copy.wait_recv()
        for s in range(1, slots):
            total = total + totals[at + s]
        at += slots
    sums_ref[...] = total
    for copy in sent:
        copy.wait_send()


def distance(k, inner):
    if k == inner:
        return 0.2
    return 1 << max(0, k - 1) if k < inner else 1 << (k - inner - 1)


def tree_stages(inner, outer):
    levels = list(range(inner + outer))
    chunks = [levels[:2]] + [levels[n : n + 3] for n in range(2, len(levels), 3)]
    stages = []
    for chunk in chunks:
        far = [k for k in chunk if k != inner]
        near = [k for k in chunk if k == inner]
        stages.append([step for step in (far, near) if step])
    return stages


def total_stages(inner, outer):
    levels = list(range(inner + outer))
    return [levels] if len(levels) <= 5 else [levels[:inner], levels[inner:]]


def update_kernel(sums_ref, x_ref, r_ref, d_ref, image_ref, x_hbm, r_hbm, d_hbm, new_x, new_r, new_d, sem):
    rr, pq, rq, qq = [sums_ref[c : c + 1, :] for c in range(4)]
    alpha = rr / pq
    fresh = rr - 2.0 * alpha * rq + alpha * alpha * qq
    nrhs = x_ref.shape[0]
    square = (nrhs, nrhs)
    diagonal = lax.broadcasted_iota(jnp.int32, square, 0) == lax.broadcasted_iota(jnp.int32, square, 1)

    def column(row):
        return jnp.sum(jnp.where(diagonal, jnp.broadcast_to(row, square), 0.0), axis=1, keepdims=True)

    step, blend = column(alpha), column(fresh / rr)
    height = nrhs // PARTS
    copies = []

    def store(n, part, src, dst):
        rows = pl.ds(part * height, height)
        copy = pltpu.make_async_copy(src.at[rows, :], dst.at[rows, :], sem.at[n, part])
        copy.start()
        copies.append(copy)

    for part in range(PARTS):
        rows = slice(part * height, (part + 1) * height)
        way = d_ref[rows, :]
        new_x[rows, :] = x_ref[rows, :] + step[rows] * way
        store(0, part, new_x, x_hbm)
        rest = r_ref[rows, :] - step[rows] * image_ref[rows, :]
        new_r[rows, :] = rest
        store(1, part, new_r, r_hbm)
        new_d[rows, :] = rest + blend[rows] * way
        store(2, part, new_d, d_hbm)
    for copy in copies:
        copy.wait()


def body(groups, leaves, points, solution, residual, direction, near, bases, leaf_transfer,
         inner_transfer, inner_coupling, outer_transfer, outer_coupling):
    leaf_dev = near.shape[0]
    leaf, rank = bases.shape[1:]
    count, dim = points.shape
    nrhs = direction.shape[1]
    rows = dim + nrhs
    inner, outer = inner_transfer.shape[0], outer_transfer.shape[0]
    stages = tree_stages(inner, outer)
    slots = max(1 << sum(len(step) for step in steps) for steps in stages)
    total_slots = sum(1 << len(order) for order in total_stages(inner, outer))
    p, x, r, d = points.T, solution.T, residual.T, direction.T
    anywhere = pl.BlockSpec(memory_space=pl.ANY)
    sems = pltpu.SemaphoreType.DMA
    whole = (nrhs, count)
    stored = (near, inner_transfer, inner_coupling, outer_transfer, outer_coupling, p, leaf_transfer, bases, d, r, x)
    stored = [pltpu.with_memory_space_constraint(a, pltpu.HBM) for a in stored]
    image, sums, d, r, x = pl.pallas_call(
        functools.partial(step_kernel, groups, leaves),
        in_specs=[anywhere] * 11,
        out_specs=[vmem] * 5,
        out_shape=[pltpu.VMEM(whole, f32), pltpu.VMEM((8, nrhs), f32)] + [pltpu.VMEM(whole, f32)] * 3,
        scratch_shapes=[
            pltpu.SMEM(near.shape, jnp.int32),
            pltpu.VMEM(inner_transfer.shape, bf16),
            pltpu.VMEM(inner_coupling.shape, bf16),
            pltpu.VMEM(outer_transfer.shape, bf16),
            pltpu.VMEM(outer_coupling.shape, bf16),
            pltpu.VMEM((rows, count), bf16),
            pltpu.VMEM((len(stages), slots * nrhs, rank), bf16),
            pltpu.VMEM((2, rows, leaf), bf16),
            pltpu.VMEM((leaf_dev + 2, leaf, 128), bf16),
            pltpu.VMEM((leaf_dev, 128, leaf), bf16),
            pltpu.VMEM(leaf_transfer.shape, bf16),
            pltpu.VMEM(bases.shape, bf16),
            pltpu.VMEM((total_slots, 8, nrhs), f32),
            sems((len(stages), slots)), sems((len(stages), slots)), sems((4,)), sems((4,)),
            sems((total_slots,)), sems((total_slots,)), sems((2 * leaf_dev + 9,)),
        ],
        compiler_params=pltpu.CompilerParams(collective_id=0, has_side_effects=True, vmem_limit_bytes=36 << 20),
        name="step",
    )(*stored)
    kept = [pltpu.with_memory_space_constraint(a, pltpu.VMEM) for a in (sums, x, r, d, image)]
    outs = pl.pallas_call(
        update_kernel,
        in_specs=[vmem] * 5,
        out_specs=[anywhere] * 3,
        out_shape=[jax.ShapeDtypeStruct(whole, f32)] * 3,
        scratch_shapes=[pltpu.VMEM(whole, f32)] * 3 + [sems((3, PARTS))],
        compiler_params=pltpu.CompilerParams(vmem_limit_bytes=16 << 20),
        name="update",
    )(*kept)
    return tuple(out.T for out in outs)


def solution(mesh):
    both = ("grp", "leaf")
    flat = P(both, None)
    deep = P(both, None, None)
    return jax.shard_map(
        functools.partial(body, mesh.shape["grp"], mesh.shape["leaf"]),
        mesh=mesh,
        in_specs=(flat, flat, flat, flat, flat, deep, deep, P(), P(), P(), P()),
        out_specs=(flat, flat, flat),
        check_vma=False,
    )
```

```python
import functools
import math

import jax
import jax.numpy as jnp
from jax import lax
from jax.experimental import pallas as pl
from jax.experimental.pallas import tpu as pltpu
from jax.sharding import PartitionSpec as P

MESH = pl.DeviceIdType.MESH
ridge = 2.0
f32 = jnp.float32
bf16 = jnp.bfloat16
vmem = pl.BlockSpec(memory_space=pltpu.VMEM)
smem = pl.BlockSpec(memory_space=pltpu.SMEM)


def nn(a, b):
    return jnp.dot(a, b, preferred_element_type=f32)


def nt(a, b):
    return lax.dot_general(a, b, (((1,), (1,)), ((), ())), preferred_element_type=f32)


def split(value):
    high = value.astype(bf16)
    low = (value - high.astype(f32)).astype(bf16)
    return jnp.concatenate([high, low], axis=0)


def fold(stacked):
    half = stacked.shape[0] // 2
    return stacked[:half] + stacked[half:]


TILE = 1024
JOBS = (('bb',), ('ob', ''))
PARTS = 4
PREP = 2
FIRST = 'pviiii'


def step_kernel(
    groups, leaves, near_hbm, inner_q_hbm, inner_b_hbm, outer_q_hbm, outer_b_hbm,
    points_hbm, trans_hbm, bases_hbm, direction_hbm, residual_hbm, solution_hbm,
    image_ref, sums_ref, direction_ref, residual_ref, solution_ref,
    near_ref, inner_q, inner_b, outer_q, outer_b, joint_ref, node_ref, halo_ref, back_ref, source, target, trans_ref, bases_ref, totals,
    node_send, node_recv, halo_send, halo_recv, total_send, total_recv, load_sem,
):
    leaf_dev, leaf = bases_ref.shape[:2]
    nrhs = image_ref.shape[0]
    dim = joint_ref.shape[0] - nrhs
    inner = inner_q.shape[0]
    outer = outer_q.shape[0]
    depth = inner + outer

    pairs = {}
    if PREP:
        pairs["points"] = (points_hbm, joint_ref.at[pl.ds(0, dim), :])
    for i in range(leaf_dev):
        cols = pl.ds(i * leaf, leaf)
        pairs["direction", i] = (direction_hbm.at[:, cols], direction_ref.at[:, cols])
        pairs["bases", i] = (bases_hbm.at[i], bases_ref.at[i])
        if i == 0:
            pairs["trans"] = (trans_hbm, trans_ref)
    if not PREP:
        pairs["points"] = (points_hbm, joint_ref.at[pl.ds(0, dim), :])
    pairs["near"] = (near_hbm, near_ref)
    pairs["iq"] = (inner_q_hbm, inner_q)
    pairs["ib"] = (inner_b_hbm, inner_b)
    pairs["oq"] = (outer_q_hbm, outer_q)
    pairs["ob"] = (outer_b_hbm, outer_b)
    pairs["residual"] = (residual_hbm, residual_ref)
    pairs["solution"] = (solution_hbm, solution_ref)
    loads = {key: pltpu.make_async_copy(a, b, load_sem.at[n]) for n, (key, (a, b)) in enumerate(pairs.items())}
    for load in loads.values():
        load.start()

    grp = lax.axis_index("grp")
    pos = lax.axis_index("leaf")
    me = grp * leaves + pos
    count = groups * leaves
    right = lax.rem(me + 1, count)
    left = lax.rem(me + count - 1, count)
    right_id = (right // leaves, lax.rem(right, leaves))
    left_id = (left // leaves, lax.rem(left, leaves))
    bits = [lax.rem(pos // (1 << k), 2) for k in range(inner)]
    bits += [lax.rem(grp // (1 << k), 2) for k in range(outer)]

    def peer(flips):
        g, p = grp, pos
        for k in flips:
            if k < inner:
                p = p + (1 - 2 * bits[k]) * (1 << k)
            else:
                g = g + (1 - 2 * bits[k]) * (1 << (k - inner))
        return g, p

    def subset(slot, order):
        return tuple(k for n, k in enumerate(order) if slot >> n & 1)

    stages = tree_stages(inner, outer)
    sum_stages = total_stages(inner, outer)

    barrier = pltpu.get_barrier_semaphore()
    met = set()
    for steps in stages:
        met |= {subset(s, step) for step in steps for s in range(1, 1 << len(step))}
    for order in sum_stages:
        met |= {subset(s, order) for s in range(1, 1 << len(order))}
    met = {tuple(sorted(flips)) for flips in met}
    greeted = [peer(flips) for flips in sorted(met)]
    if len(met) < count - 1:
        greeted += [left_id, right_id]
    for who in greeted:
        pl.semaphore_signal(barrier, inc=1, device_id=who, device_id_type=MESH)

    def ship(n, src, dst, who):
        return pltpu.make_async_remote_copy(
            src_ref=src, dst_ref=dst, send_sem=halo_send.at[n], recv_sem=halo_recv.at[n],
            device_id=who, device_id_type=MESH,
        )

    halo_points = ship(0, joint_ref.at[pl.ds(0, dim), pl.ds(0, leaf)], halo_ref.at[pl.ds(0, dim), :], left_id)
    halo_values = ship(1, joint_ref.at[pl.ds(dim, nrhs), pl.ds(0, leaf)], halo_ref.at[pl.ds(dim, nrhs), :], left_id)
    pieces = [pl.ds(t * (leaf // 2), leaf // 2) for t in range(2)]
    halo_back = [ship(2 + t, back_ref.at[0, :, cols], back_ref.at[1, :, cols], right_id) for t, cols in enumerate(pieces)]

    def prepare(i):
        wide, extra = parts(joint_ref[:dim, i * leaf : (i + 1) * leaf])
        put_source(i, wide, extra)
        target[i] = jnp.concatenate([wide, extra(3, 0)], axis=0).astype(bf16)

    tile = min(leaf, TILE)
    scale = 2.0 / dim * math.log2(math.e)

    def parts(pts):
        wide = pts.astype(f32)
        sq = jnp.sum(wide * wide, axis=0, keepdims=True)
        high = sq.astype(bf16).astype(f32)
        mid = (sq - high).astype(bf16).astype(f32)
        low = sq - high - mid
        row = lax.broadcasted_iota(jnp.int32, (128 - dim, pts.shape[1]), 0)

        def extra(first, second):
            ones = jnp.where(jnp.logical_and(row >= second, row < second + 3), 1.0, 0.0)
            return jnp.where(row == first, -high, jnp.where(row == first + 1, -mid, jnp.where(row == first + 2, -low, ones)))

        return wide, extra

    def put_source(slot, wide, extra):
        source[slot] = jnp.concatenate([2.0 * wide, extra(0, 3)], axis=0).T.astype(bf16)

    early = [(leaf_dev - 1 + n) % leaf_dev for n in range(PREP)]
    if PREP:
        loads["points"].wait()
    for i in early:
        prepare(i)

    node = None
    for i in range(leaf_dev):
        cols = slice(i * leaf, (i + 1) * leaf)
        loads["direction", i].wait()
        joint_ref[dim:, cols] = direction_ref[:, cols].astype(bf16)
        loads["bases", i].wait()
        skel = nn(joint_ref[dim:, cols], bases_ref[i])
        if i == 0:
            loads["trans"].wait()
        term = nn(split(skel), trans_ref[i])
        node = term if node is None else node + term
    node = fold(node)

    def block(i, slot, values):
        acc = jnp.zeros((nrhs, leaf), f32)
        for t in range(leaf // tile):
            power = nn(source[slot, t * tile : (t + 1) * tile, :], target[i])
            kern = jnp.exp2(power * scale).astype(bf16)
            acc += nn(values(t), kern)
        return acc

    def own(j):
        return lambda t: joint_ref[dim:, j * leaf + t * tile : j * leaf + (t + 1) * tile]

    def itself(i):
        cols = slice(i * leaf, (i + 1) * leaf)
        if i not in early:
            prepare(i)
        image_ref[:, cols] = ridge * direction_ref[:, cols] + block(i, i, own(i))

    def beside(i):
        here = jnp.where(near_ref[i, 2] >= 0, 1.0, 0.0).astype(f32)
        there = jnp.where(near_ref[i + 1, 1] >= 0, 1.0, 0.0).astype(f32)
        mine = joint_ref[dim:, i * leaf : (i + 1) * leaf]
        values = own(i + 1)
        acc = jnp.zeros((nrhs, leaf), f32)
        for t in range(leaf // tile):
            power = nn(source[i + 1, t * tile : (t + 1) * tile, :], target[i])
            kern = jnp.exp2(power * scale).astype(bf16)
            acc += nn(values(t), kern)
            cols = slice((i + 1) * leaf + t * tile, (i + 1) * leaf + (t + 1) * tile)
            image_ref[:, cols] += there * nt(mine, kern)
        image_ref[:, i * leaf : (i + 1) * leaf] += here * acc

    def outside():
        i = leaf_dev - 1
        halo_points.wait_recv()
        put_source(leaf_dev, *parts(halo_ref[:dim, :]))
        halo_values.wait_recv()
        here = jnp.where(near_ref[i, 2] >= 0, 1.0, 0.0).astype(f32)
        mine = joint_ref[dim:, i * leaf : (i + 1) * leaf]
        acc = jnp.zeros((nrhs, leaf), f32)
        for t, copy in enumerate(halo_back):
            cols = slice(t * (leaf // 2), (t + 1) * (leaf // 2))
            power = nn(source[leaf_dev, cols, :], target[i])
            kern = jnp.exp2(power * scale).astype(bf16)
            back_ref[0, :, cols] = nt(mine, kern).astype(bf16)
            copy.start()
            acc += nn(halo_ref[dim:, cols], kern)
        image_ref[:, i * leaf : (i + 1) * leaf] += here * acc

    def returned():
        for copy in halo_back:
            copy.wait_recv()
        there = jnp.where(near_ref[0, 1] >= 0, 1.0, 0.0).astype(f32)
        image_ref[:, :leaf] += there * back_ref[1].astype(f32)

    def narrow(value):
        out = value[:, :128]
        for c in range(1, value.shape[1] // 128):
            out += value[:, c * 128 : (c + 1) * 128]
        return out

    def squares():
        loads["residual"].wait()
        total = jnp.zeros((nrhs, 128), f32)
        for i in range(leaf_dev):
            rest = residual_ref[:, i * leaf : (i + 1) * leaf]
            total = total + narrow(rest * rest)
        return jnp.sum(total.T, axis=0, keepdims=True)

    plan = {"o": [outside], "p": [halo_points.start], "v": [halo_values.start]}
    plan["i"] = [functools.partial(itself, (leaf_dev - 1 + n) % leaf_dev) for n in range(leaf_dev)]
    plan["b"] = [functools.partial(beside, i) for i in range(leaf_dev - 1)]

    def work(kinds):
        for kind in kinds:
            if plan[kind]:
                plan[kind].pop(0)()

    def finish():
        for kind in "pviob":
            while plan[kind]:
                plan[kind].pop(0)()

    pl.semaphore_wait(barrier, len(greeted))
    work("pv" if "v" in FIRST else "")
    if not PREP:
        loads["points"].wait()
    loads["near"].wait()

    def tables(k):
        return (inner_q, inner_b, k) if k < inner else (outer_q, outer_b, k - inner)

    def rows_of(pieces):
        return jnp.concatenate(pieces, axis=0) if len(pieces) > 1 else pieces[0]

    def product(groups_of_pieces, matrix, op):
        flat = [piece for pieces in groups_of_pieces for piece in pieces]
        out = op(rows_of(flat), matrix)
        sums, at = [], 0
        for pieces in groups_of_pieces:
            total = None
            for _ in pieces:
                part = out[at * nrhs : (at + 1) * nrhs]
                total = part if total is None else total + part
                at += 1
            sums.append(total)
        return sums

    def pair(value):
        high = value.astype(bf16)
        return [high, (value - high.astype(f32)).astype(bf16)]

    work(FIRST)
    records = []
    sent = []
    for c, steps in enumerate(stages):
        order = [k for step in steps for k in step]
        node_ref[c, :nrhs] = node.astype(bf16)
        held = 1
        for n, step in enumerate(steps):
            copies = []
            for s in range(1, 1 << len(step)):
                copies.append(pltpu.make_async_remote_copy(
                    src_ref=node_ref.at[c, pl.ds(0, held * nrhs), :],
                    dst_ref=node_ref.at[c, pl.ds(s * held * nrhs, held * nrhs), :],
                    send_sem=node_send.at[c, s * held], recv_sem=node_recv.at[c, s * held],
                    device_id=peer(subset(s, step)), device_id_type=MESH,
                ))
            for copy in reversed(copies):
                copy.start()
            if (c, n) == (0, 0):
                for key in ("iq", "ib", "oq", "ob"):
                    loads[key].wait()
            work(JOBS[c][n] if c < len(JOBS) and n < len(JOBS[c]) else "")
            for copy in copies:
                copy.wait_recv()
            sent += copies
            held <<= len(step)
        current = {s: [node_ref[c, s * nrhs : (s + 1) * nrhs]] for s in range(1, held)}
        current[0] = pair(node)
        final = c == len(stages) - 1
        for k in sorted(order):
            b = 1 << order.index(k)
            q_ref, b_ref, index = tables(k)
            mat = b_ref[index]
            sibling = [current[b]]
            records.append(jnp.where(bits[k] == 0, product(sibling, mat, nt)[0], product(sibling, mat, nn)[0]))
            low = [s for s in sorted(current) if not s & b and not (final and s == 0)]
            if low:
                mine = product([current[s] for s in low], q_ref[index, bits[k]], nn)
                other = product([current[s | b] for s in low], q_ref[index, 1 - bits[k]], nn)
                merged = {s: x + y for s, x, y in zip(low, mine, other)}
            else:
                merged = {}
            if not final:
                node = merged[0]
            current = {s: pair(v) for s, v in merged.items()}

    incoming = records[-1]
    for k in reversed(range(depth - 1)):
        q_ref, _, index = tables(k)
        incoming = records[k] + product([pair(incoming)], q_ref[index, bits[k]], nt)[0]

    stacked = split(incoming)
    inputs = [fold(nt(stacked, trans_ref[i])).astype(bf16) for i in range(leaf_dev)]
    finish()
    rr = squares()
    loads["solution"].wait()
    sums = [jnp.zeros((nrhs, 128), f32)] * 3
    for i in reversed(range(leaf_dev)):
        if i == 0:
            returned()
        cols = slice(i * leaf, (i + 1) * leaf)
        image = image_ref[:, cols] + nt(inputs[i], bases_ref[i])
        image_ref[:, cols] = image
        terms = (direction_ref[:, cols] * image, residual_ref[:, cols] * image, image * image)
        sums = [s + narrow(t) for s, t in zip(sums, terms)]
    rows = [rr] + [jnp.sum(s.T, axis=0, keepdims=True) for s in sums]
    total = jnp.concatenate(rows + [jnp.zeros((4, nrhs), f32)], axis=0)

    at = 0
    for order in sum_stages:
        slots = 1 << len(order)
        totals[at] = total
        copies = []
        for s in sorted(range(1, slots), key=lambda s: -sum(distance(k, inner) for k in subset(s, order))):
            copies.append(pltpu.make_async_remote_copy(
                src_ref=totals.at[at], dst_ref=totals.at[at + s],
                send_sem=total_send.at[at + s], recv_sem=total_recv.at[at + s],
                device_id=peer(subset(s, order)), device_id_type=MESH,
            ))
        for copy in copies:
            copy.start()
        sent += copies
        for copy in reversed(copies):
            copy.wait_recv()
        for s in range(1, slots):
            total = total + totals[at + s]
        at += slots
    sums_ref[...] = total
    for copy in sent + [halo_points, halo_values] + halo_back:
        copy.wait_send()


def distance(k, inner):
    if k == inner:
        return 0.2
    return 1 << max(0, k - 1) if k < inner else 1 << (k - inner - 1)


def tree_stages(inner, outer):
    levels = list(range(inner + outer))
    chunks = [levels[:2]] + [levels[n : n + 3] for n in range(2, len(levels), 3)]
    stages = []
    for chunk in chunks:
        far = [k for k in chunk if k != inner]
        near = [k for k in chunk if k == inner]
        stages.append([step for step in (far, near) if step])
    return stages


def total_stages(inner, outer):
    levels = list(range(inner + outer))
    return [levels] if len(levels) <= 5 else [levels[:inner], levels[inner:]]


def update_kernel(sums_ref, x_ref, r_ref, d_ref, image_ref, x_hbm, r_hbm, d_hbm, new_x, new_r, new_d, sem):
    rr, pq, rq, qq = [sums_ref[c : c + 1, :] for c in range(4)]
    alpha = rr / pq
    fresh = rr - 2.0 * alpha * rq + alpha * alpha * qq
    nrhs = x_ref.shape[0]
    square = (nrhs, nrhs)
    diagonal = lax.broadcasted_iota(jnp.int32, square, 0) == lax.broadcasted_iota(jnp.int32, square, 1)

    def column(row):
        return jnp.sum(jnp.where(diagonal, jnp.broadcast_to(row, square), 0.0), axis=1, keepdims=True)

    step, blend = column(alpha), column(fresh / rr)
    height = nrhs // PARTS
    copies = []

    def store(n, part, src, dst):
        rows = pl.ds(part * height, height)
        copy = pltpu.make_async_copy(src.at[rows, :], dst.at[rows, :], sem.at[n, part])
        copy.start()
        copies.append(copy)

    for part in range(PARTS):
        rows = slice(part * height, (part + 1) * height)
        way = d_ref[rows, :]
        new_x[rows, :] = x_ref[rows, :] + step[rows] * way
        store(0, part, new_x, x_hbm)
        rest = r_ref[rows, :] - step[rows] * image_ref[rows, :]
        new_r[rows, :] = rest
        store(1, part, new_r, r_hbm)
        new_d[rows, :] = rest + blend[rows] * way
        store(2, part, new_d, d_hbm)
    for copy in copies:
        copy.wait()


def body(groups, leaves, points, solution, residual, direction, near, bases, leaf_transfer,
         inner_transfer, inner_coupling, outer_transfer, outer_coupling):
    leaf_dev = near.shape[0]
    leaf, rank = bases.shape[1:]
    count, dim = points.shape
    nrhs = direction.shape[1]
    rows = dim + nrhs
    inner, outer = inner_transfer.shape[0], outer_transfer.shape[0]
    stages = tree_stages(inner, outer)
    slots = max(1 << sum(len(step) for step in steps) for steps in stages)
    total_slots = sum(1 << len(order) for order in total_stages(inner, outer))
    p, x, r, d = points.T, solution.T, residual.T, direction.T
    anywhere = pl.BlockSpec(memory_space=pl.ANY)
    sems = pltpu.SemaphoreType.DMA
    whole = (nrhs, count)
    stored = (near, inner_transfer, inner_coupling, outer_transfer, outer_coupling, p, leaf_transfer, bases, d, r, x)
    stored = [pltpu.with_memory_space_constraint(a, pltpu.HBM) for a in stored]
    image, sums, d, r, x = pl.pallas_call(
        functools.partial(step_kernel, groups, leaves),
        in_specs=[anywhere] * 11,
        out_specs=[vmem] * 5,
        out_shape=[pltpu.VMEM(whole, f32), pltpu.VMEM((8, nrhs), f32)] + [pltpu.VMEM(whole, f32)] * 3,
        scratch_shapes=[
            pltpu.SMEM(near.shape, jnp.int32),
            pltpu.VMEM(inner_transfer.shape, bf16),
            pltpu.VMEM(inner_coupling.shape, bf16),
            pltpu.VMEM(outer_transfer.shape, bf16),
            pltpu.VMEM(outer_coupling.shape, bf16),
            pltpu.VMEM((rows, count), bf16),
            pltpu.VMEM((len(stages), slots * nrhs, rank), bf16),
            pltpu.VMEM((rows, leaf), bf16),
            pltpu.VMEM((2, nrhs, leaf), bf16),
            pltpu.VMEM((leaf_dev + 1, leaf, 128), bf16),
            pltpu.VMEM((leaf_dev, 128, leaf), bf16),
            pltpu.VMEM(leaf_transfer.shape, bf16),
            pltpu.VMEM(bases.shape, bf16),
            pltpu.VMEM((total_slots, 8, nrhs), f32),
            sems((len(stages), slots)), sems((len(stages), slots)), sems((4,)), sems((4,)),
            sems((total_slots,)), sems((total_slots,)), sems((2 * leaf_dev + 9,)),
        ],
        compiler_params=pltpu.CompilerParams(collective_id=0, has_side_effects=True, vmem_limit_bytes=36 << 20),
        name="step",
    )(*stored)
    kept = [pltpu.with_memory_space_constraint(a, pltpu.VMEM) for a in (sums, x, r, d, image)]
    outs = pl.pallas_call(
        update_kernel,
        in_specs=[vmem] * 5,
        out_specs=[anywhere] * 3,
        out_shape=[jax.ShapeDtypeStruct(whole, f32)] * 3,
        scratch_shapes=[pltpu.VMEM(whole, f32)] * 3 + [sems((3, PARTS))],
        compiler_params=pltpu.CompilerParams(vmem_limit_bytes=16 << 20),
        name="update",
    )(*kept)
    return tuple(out.T for out in outs)


def solution(mesh):
    both = ("grp", "leaf")
    flat = P(both, None)
    deep = P(both, None, None)
    return jax.shard_map(
        functools.partial(body, mesh.shape["grp"], mesh.shape["leaf"]),
        mesh=mesh,
        in_specs=(flat, flat, flat, flat, flat, deep, deep, P(), P(), P(), P()),
        out_specs=(flat, flat, flat),
        check_vma=False,
    )
```

```python
import functools
import math

import jax
import jax.numpy as jnp
from jax import lax
from jax.experimental import pallas as pl
from jax.experimental.pallas import tpu as pltpu
from jax.sharding import PartitionSpec as P

MESH = pl.DeviceIdType.MESH
ridge = 2.0
f32 = jnp.float32
bf16 = jnp.bfloat16
vmem = pl.BlockSpec(memory_space=pltpu.VMEM)
smem = pl.BlockSpec(memory_space=pltpu.SMEM)


def nn(a, b):
    return jnp.dot(a, b, preferred_element_type=f32)


def nt(a, b):
    return lax.dot_general(a, b, (((1,), (1,)), ((), ())), preferred_element_type=f32)


def split(value):
    high = value.astype(bf16)
    low = (value - high.astype(f32)).astype(bf16)
    return jnp.concatenate([high, low], axis=0)


def fold(stacked):
    half = stacked.shape[0] // 2
    return stacked[:half] + stacked[half:]


TILE = 1024
JOBS = (('ibb',), ('ob', ''))
PARTS = 4
PREP = 2
BAR = 2
LATER = True
FIRST = 'iii'


def step_kernel(
    groups, leaves, near_hbm, inner_q_hbm, inner_b_hbm, outer_q_hbm, outer_b_hbm,
    points_hbm, trans_hbm, bases_hbm, direction_hbm, residual_hbm, solution_hbm,
    image_ref, sums_ref, direction_ref, residual_ref, solution_ref,
    near_ref, inner_q, inner_b, outer_q, outer_b, joint_ref, node_ref, halo_ref, back_ref, source, target, trans_ref, bases_ref, totals,
    node_send, node_recv, halo_send, halo_recv, total_send, total_recv, load_sem,
):
    leaf_dev, leaf = bases_ref.shape[:2]
    nrhs = image_ref.shape[0]
    dim = joint_ref.shape[1] - nrhs
    inner = inner_q.shape[0]
    outer = outer_q.shape[0]
    depth = inner + outer

    pairs = {}
    for i in range(leaf_dev):
        pairs["points", i] = (points_hbm.at[:, pl.ds(i * leaf, leaf)], joint_ref.at[i, pl.ds(0, dim), :])
    for i in range(leaf_dev):
        cols = pl.ds(i * leaf, leaf)
        pairs["direction", i] = (direction_hbm.at[:, cols], direction_ref.at[:, cols])
        pairs["bases", i] = (bases_hbm.at[i], bases_ref.at[i])
        if i == 0:
            pairs["trans"] = (trans_hbm, trans_ref)
    pairs["near"] = (near_hbm, near_ref)
    pairs["iq"] = (inner_q_hbm, inner_q)
    pairs["ib"] = (inner_b_hbm, inner_b)
    pairs["oq"] = (outer_q_hbm, outer_q)
    pairs["ob"] = (outer_b_hbm, outer_b)
    pairs["residual"] = (residual_hbm, residual_ref)
    pairs["solution"] = (solution_hbm, solution_ref)
    loads = {key: pltpu.make_async_copy(a, b, load_sem.at[n]) for n, (key, (a, b)) in enumerate(pairs.items())}
    later = ("iq", "ib", "oq", "ob", "residual", "solution") if LATER else ()
    for key, load in loads.items():
        if key not in later:
            load.start()

    grp = lax.axis_index("grp")
    pos = lax.axis_index("leaf")
    me = grp * leaves + pos
    count = groups * leaves
    right = lax.rem(me + 1, count)
    left = lax.rem(me + count - 1, count)
    right_id = (right // leaves, lax.rem(right, leaves))
    left_id = (left // leaves, lax.rem(left, leaves))
    bits = [lax.rem(pos // (1 << k), 2) for k in range(inner)]
    bits += [lax.rem(grp // (1 << k), 2) for k in range(outer)]

    def peer(flips):
        g, p = grp, pos
        for k in flips:
            if k < inner:
                p = p + (1 - 2 * bits[k]) * (1 << k)
            else:
                g = g + (1 - 2 * bits[k]) * (1 << (k - inner))
        return g, p

    def subset(slot, order):
        return tuple(k for n, k in enumerate(order) if slot >> n & 1)

    stages = tree_stages(inner, outer)
    sum_stages = total_stages(inner, outer)

    barrier = pltpu.get_barrier_semaphore()
    met = set()
    for steps in stages:
        met |= {subset(s, step) for step in steps for s in range(1, 1 << len(step))}
    for order in sum_stages:
        met |= {subset(s, order) for s in range(1, 1 << len(order))}
    met = {tuple(sorted(flips)) for flips in met}
    greeted = [peer(flips) for flips in sorted(met)]
    if len(met) < count - 1:
        greeted += [left_id, right_id]
    for who in greeted:
        pl.semaphore_signal(barrier, inc=1, device_id=who, device_id_type=MESH)

    def ship(n, src, dst, who):
        return pltpu.make_async_remote_copy(
            src_ref=src, dst_ref=dst, send_sem=halo_send.at[n], recv_sem=halo_recv.at[n],
            device_id=who, device_id_type=MESH,
        )

    halo_points = ship(0, joint_ref.at[0, pl.ds(0, dim), :], halo_ref.at[pl.ds(0, dim), :], left_id)
    halo_values = ship(1, joint_ref.at[0, pl.ds(dim, nrhs), :], halo_ref.at[pl.ds(dim, nrhs), :], left_id)
    halo_back = [ship(2 + t, back_ref.at[t], back_ref.at[2 + t], right_id) for t in range(2)]

    def prepare(i):
        wide, extra = parts(joint_ref[i, :dim, :])
        put_source(i, wide, extra)
        target[i] = jnp.concatenate([wide, extra(3, 0)], axis=0).astype(bf16)

    tile = min(leaf, TILE)
    scale = 2.0 / dim * math.log2(math.e)

    def parts(pts):
        wide = pts.astype(f32)
        sq = jnp.sum(wide * wide, axis=0, keepdims=True)
        high = sq.astype(bf16).astype(f32)
        mid = (sq - high).astype(bf16).astype(f32)
        low = sq - high - mid
        row = lax.broadcasted_iota(jnp.int32, (128 - dim, pts.shape[1]), 0)

        def extra(first, second):
            ones = jnp.where(jnp.logical_and(row >= second, row < second + 3), 1.0, 0.0)
            return jnp.where(row == first, -high, jnp.where(row == first + 1, -mid, jnp.where(row == first + 2, -low, ones)))

        return wide, extra

    def put_source(slot, wide, extra):
        source[slot] = jnp.concatenate([2.0 * wide, extra(0, 3)], axis=0).T.astype(bf16)

    early = [(leaf_dev - 1 + n) % leaf_dev for n in range(PREP)]
    for i in range(leaf_dev):
        loads["points", i].wait()
    for i in early:
        prepare(i)

    node = None
    for i in range(leaf_dev):
        cols = slice(i * leaf, (i + 1) * leaf)
        loads["direction", i].wait()
        joint_ref[i, dim:, :] = direction_ref[:, cols].astype(bf16)
        if i == BAR:
            pl.semaphore_wait(barrier, len(greeted))
            halo_points.start()
            halo_values.start()
        loads["bases", i].wait()
        skel = nn(joint_ref[i, dim:, :], bases_ref[i])
        if i == 0:
            loads["trans"].wait()
        term = nn(split(skel), trans_ref[i])
        node = term if node is None else node + term
    for key in later:
        loads[key].start()
    node = fold(node)

    def block(i, slot, values):
        acc = jnp.zeros((nrhs, leaf), f32)
        for t in range(leaf // tile):
            power = nn(source[slot, t * tile : (t + 1) * tile, :], target[i])
            kern = jnp.exp2(power * scale).astype(bf16)
            acc += nn(values(t), kern)
        return acc

    def own(j):
        return lambda t: joint_ref[j, dim:, t * tile : (t + 1) * tile]

    def itself(i):
        cols = slice(i * leaf, (i + 1) * leaf)
        if i not in early:
            prepare(i)
        image_ref[:, cols] = ridge * direction_ref[:, cols] + block(i, i, own(i))

    def beside(i):
        here = jnp.where(near_ref[i, 2] >= 0, 1.0, 0.0).astype(f32)
        there = jnp.where(near_ref[i + 1, 1] >= 0, 1.0, 0.0).astype(f32)
        mine = joint_ref[i, dim:, :]
        values = own(i + 1)
        acc = jnp.zeros((nrhs, leaf), f32)
        for t in range(leaf // tile):
            power = nn(source[i + 1, t * tile : (t + 1) * tile, :], target[i])
            kern = jnp.exp2(power * scale).astype(bf16)
            acc += nn(values(t), kern)
            cols = slice((i + 1) * leaf + t * tile, (i + 1) * leaf + (t + 1) * tile)
            image_ref[:, cols] += there * nt(mine, kern)
        image_ref[:, i * leaf : (i + 1) * leaf] += here * acc

    def outside():
        i = leaf_dev - 1
        halo_points.wait_recv()
        put_source(leaf_dev, *parts(halo_ref[:dim, :]))
        halo_values.wait_recv()
        here = jnp.where(near_ref[i, 2] >= 0, 1.0, 0.0).astype(f32)
        mine = joint_ref[i, dim:, :]
        acc = jnp.zeros((nrhs, leaf), f32)
        for t, copy in enumerate(halo_back):
            cols = slice(t * (leaf // 2), (t + 1) * (leaf // 2))
            power = nn(source[leaf_dev, cols, :], target[i])
            kern = jnp.exp2(power * scale).astype(bf16)
            back_ref[t] = nt(mine, kern).astype(bf16)
            copy.start()
            acc += nn(halo_ref[dim:, cols], kern)
        image_ref[:, i * leaf : (i + 1) * leaf] += here * acc

    def returned():
        for copy in halo_back:
            copy.wait_recv()
        there = jnp.where(near_ref[0, 1] >= 0, 1.0, 0.0).astype(f32)
        image_ref[:, : leaf // 2] += there * back_ref[2].astype(f32)
        image_ref[:, leaf // 2 : leaf] += there * back_ref[3].astype(f32)

    def narrow(value):
        out = value[:, :128]
        for c in range(1, value.shape[1] // 128):
            out += value[:, c * 128 : (c + 1) * 128]
        return out

    def squares():
        loads["residual"].wait()
        total = jnp.zeros((nrhs, 128), f32)
        for i in range(leaf_dev):
            rest = residual_ref[:, i * leaf : (i + 1) * leaf]
            total = total + narrow(rest * rest)
        return jnp.sum(total.T, axis=0, keepdims=True)

    plan = {"o": [outside]}
    plan["i"] = [functools.partial(itself, (leaf_dev - 1 + n) % leaf_dev) for n in range(leaf_dev)]
    plan["b"] = [functools.partial(beside, i) for i in range(leaf_dev - 1)]

    def work(kinds):
        for kind in kinds:
            if plan[kind]:
                plan[kind].pop(0)()

    def finish():
        for kind in "iob":
            while plan[kind]:
                plan[kind].pop(0)()

    if BAR >= leaf_dev:
        pl.semaphore_wait(barrier, len(greeted))
        halo_points.start()
        halo_values.start()
    loads["near"].wait()

    def tables(k):
        return (inner_q, inner_b, k) if k < inner else (outer_q, outer_b, k - inner)

    def rows_of(pieces):
        return jnp.concatenate(pieces, axis=0) if len(pieces) > 1 else pieces[0]

    def product(groups_of_pieces, matrix, op):
        flat = [piece for pieces in groups_of_pieces for piece in pieces]
        out = op(rows_of(flat), matrix)
        sums, at = [], 0
        for pieces in groups_of_pieces:
            total = None
            for _ in pieces:
                part = out[at * nrhs : (at + 1) * nrhs]
                total = part if total is None else total + part
                at += 1
            sums.append(total)
        return sums

    def pair(value):
        high = value.astype(bf16)
        return [high, (value - high.astype(f32)).astype(bf16)]

    work(FIRST)
    records = []
    sent = []
    for c, steps in enumerate(stages):
        order = [k for step in steps for k in step]
        node_ref[c, :nrhs] = node.astype(bf16)
        held = 1
        for n, step in enumerate(steps):
            copies = []
            for s in range(1, 1 << len(step)):
                copies.append(pltpu.make_async_remote_copy(
                    src_ref=node_ref.at[c, pl.ds(0, held * nrhs), :],
                    dst_ref=node_ref.at[c, pl.ds(s * held * nrhs, held * nrhs), :],
                    send_sem=node_send.at[c, s * held], recv_sem=node_recv.at[c, s * held],
                    device_id=peer(subset(s, step)), device_id_type=MESH,
                ))
            for copy in reversed(copies):
                copy.start()
            if (c, n) == (0, 0):
                for key in ("iq", "ib", "oq", "ob"):
                    loads[key].wait()
            work(JOBS[c][n] if c < len(JOBS) and n < len(JOBS[c]) else "")
            for copy in copies:
                copy.wait_recv()
            sent += copies
            held <<= len(step)
        current = {s: [node_ref[c, s * nrhs : (s + 1) * nrhs]] for s in range(1, held)}
        current[0] = pair(node)
        final = c == len(stages) - 1
        for k in sorted(order):
            b = 1 << order.index(k)
            q_ref, b_ref, index = tables(k)
            mat = b_ref[index]
            sibling = [current[b]]
            records.append(jnp.where(bits[k] == 0, product(sibling, mat, nt)[0], product(sibling, mat, nn)[0]))
            low = [s for s in sorted(current) if not s & b and not (final and s == 0)]
            if low:
                mine = product([current[s] for s in low], q_ref[index, bits[k]], nn)
                other = product([current[s | b] for s in low], q_ref[index, 1 - bits[k]], nn)
                merged = {s: x + y for s, x, y in zip(low, mine, other)}
            else:
                merged = {}
            if not final:
                node = merged[0]
            current = {s: pair(v) for s, v in merged.items()}

    incoming = records[-1]
    for k in reversed(range(depth - 1)):
        q_ref, _, index = tables(k)
        incoming = records[k] + product([pair(incoming)], q_ref[index, bits[k]], nt)[0]

    stacked = split(incoming)
    inputs = [fold(nt(stacked, trans_ref[i])).astype(bf16) for i in range(leaf_dev)]
    finish()
    rr = squares()
    loads["solution"].wait()
    sums = [jnp.zeros((nrhs, 128), f32)] * 3
    for i in reversed(range(leaf_dev)):
        if i == 0:
            returned()
        cols = slice(i * leaf, (i + 1) * leaf)
        image = image_ref[:, cols] + nt(inputs[i], bases_ref[i])
        image_ref[:, cols] = image
        terms = (direction_ref[:, cols] * image, residual_ref[:, cols] * image, image * image)
        sums = [s + narrow(t) for s, t in zip(sums, terms)]
    rows = [rr] + [jnp.sum(s.T, axis=0, keepdims=True) for s in sums]
    total = jnp.concatenate(rows + [jnp.zeros((4, nrhs), f32)], axis=0)

    at = 0
    for order in sum_stages:
        slots = 1 << len(order)
        totals[at] = total
        copies = []
        for s in sorted(range(1, slots), key=lambda s: -sum(distance(k, inner) for k in subset(s, order))):
            copies.append(pltpu.make_async_remote_copy(
                src_ref=totals.at[at], dst_ref=totals.at[at + s],
                send_sem=total_send.at[at + s], recv_sem=total_recv.at[at + s],
                device_id=peer(subset(s, order)), device_id_type=MESH,
            ))
        for copy in copies:
            copy.start()
        sent += copies
        for copy in reversed(copies):
            copy.wait_recv()
        for s in range(1, slots):
            total = total + totals[at + s]
        at += slots
    sums_ref[...] = total
    for copy in sent + [halo_points, halo_values] + halo_back:
        copy.wait_send()


def distance(k, inner):
    if k == inner:
        return 0.2
    return 1 << max(0, k - 1) if k < inner else 1 << (k - inner - 1)


def tree_stages(inner, outer):
    levels = list(range(inner + outer))
    chunks = [levels[:2]] + [levels[n : n + 3] for n in range(2, len(levels), 3)]
    stages = []
    for chunk in chunks:
        far = [k for k in chunk if k != inner]
        near = [k for k in chunk if k == inner]
        stages.append([step for step in (far, near) if step])
    return stages


def total_stages(inner, outer):
    levels = list(range(inner + outer))
    return [levels] if len(levels) <= 5 else [levels[:inner], levels[inner:]]


def update_kernel(sums_ref, x_ref, r_ref, d_ref, image_ref, x_hbm, r_hbm, d_hbm, new_x, new_r, new_d, sem):
    rr, pq, rq, qq = [sums_ref[c : c + 1, :] for c in range(4)]
    alpha = rr / pq
    fresh = rr - 2.0 * alpha * rq + alpha * alpha * qq
    nrhs = x_ref.shape[0]
    square = (nrhs, nrhs)
    diagonal = lax.broadcasted_iota(jnp.int32, square, 0) == lax.broadcasted_iota(jnp.int32, square, 1)

    def column(row):
        return jnp.sum(jnp.where(diagonal, jnp.broadcast_to(row, square), 0.0), axis=1, keepdims=True)

    step, blend = column(alpha), column(fresh / rr)
    height = nrhs // PARTS
    copies = []

    def store(n, part, src, dst):
        rows = pl.ds(part * height, height)
        copy = pltpu.make_async_copy(src.at[rows, :], dst.at[rows, :], sem.at[n, part])
        copy.start()
        copies.append(copy)

    for part in range(PARTS):
        rows = slice(part * height, (part + 1) * height)
        way = d_ref[rows, :]
        new_x[rows, :] = x_ref[rows, :] + step[rows] * way
        store(0, part, new_x, x_hbm)
        rest = r_ref[rows, :] - step[rows] * image_ref[rows, :]
        new_r[rows, :] = rest
        store(1, part, new_r, r_hbm)
        new_d[rows, :] = rest + blend[rows] * way
        store(2, part, new_d, d_hbm)
    for copy in copies:
        copy.wait()


def body(groups, leaves, points, solution, residual, direction, near, bases, leaf_transfer,
         inner_transfer, inner_coupling, outer_transfer, outer_coupling):
    leaf_dev = near.shape[0]
    leaf, rank = bases.shape[1:]
    count, dim = points.shape
    nrhs = direction.shape[1]
    rows = dim + nrhs
    inner, outer = inner_transfer.shape[0], outer_transfer.shape[0]
    stages = tree_stages(inner, outer)
    slots = max(1 << sum(len(step) for step in steps) for steps in stages)
    total_slots = sum(1 << len(order) for order in total_stages(inner, outer))
    p, x, r, d = points.T, solution.T, residual.T, direction.T
    anywhere = pl.BlockSpec(memory_space=pl.ANY)
    sems = pltpu.SemaphoreType.DMA
    whole = (nrhs, count)
    stored = (near, inner_transfer, inner_coupling, outer_transfer, outer_coupling, p, leaf_transfer, bases, d, r, x)
    stored = [pltpu.with_memory_space_constraint(a, pltpu.HBM) for a in stored]
    image, sums, d, r, x = pl.pallas_call(
        functools.partial(step_kernel, groups, leaves),
        in_specs=[anywhere] * 11,
        out_specs=[vmem] * 5,
        out_shape=[pltpu.VMEM(whole, f32), pltpu.VMEM((8, nrhs), f32)] + [pltpu.VMEM(whole, f32)] * 3,
        scratch_shapes=[
            pltpu.SMEM(near.shape, jnp.int32),
            pltpu.VMEM(inner_transfer.shape, bf16),
            pltpu.VMEM(inner_coupling.shape, bf16),
            pltpu.VMEM(outer_transfer.shape, bf16),
            pltpu.VMEM(outer_coupling.shape, bf16),
            pltpu.VMEM((leaf_dev, rows, leaf), bf16),
            pltpu.VMEM((len(stages), slots * nrhs, rank), bf16),
            pltpu.VMEM((rows, leaf), bf16),
            pltpu.VMEM((4, nrhs, leaf // 2), bf16),
            pltpu.VMEM((leaf_dev + 1, leaf, 128), bf16),
            pltpu.VMEM((leaf_dev, 128, leaf), bf16),
            pltpu.VMEM(leaf_transfer.shape, bf16),
            pltpu.VMEM(bases.shape, bf16),
            pltpu.VMEM((total_slots, 8, nrhs), f32),
            sems((len(stages), slots)), sems((len(stages), slots)), sems((4,)), sems((4,)),
            sems((total_slots,)), sems((total_slots,)), sems((3 * leaf_dev + 9,)),
        ],
        compiler_params=pltpu.CompilerParams(collective_id=0, has_side_effects=True, vmem_limit_bytes=36 << 20),
        name="step",
    )(*stored)
    kept = [pltpu.with_memory_space_constraint(a, pltpu.VMEM) for a in (sums, x, r, d, image)]
    outs = pl.pallas_call(
        update_kernel,
        in_specs=[vmem] * 5,
        out_specs=[anywhere] * 3,
        out_shape=[jax.ShapeDtypeStruct(whole, f32)] * 3,
        scratch_shapes=[pltpu.VMEM(whole, f32)] * 3 + [sems((3, PARTS))],
        compiler_params=pltpu.CompilerParams(vmem_limit_bytes=16 << 20),
        name="update",
    )(*kept)
    return tuple(out.T for out in outs)


def solution(mesh):
    both = ("grp", "leaf")
    flat = P(both, None)
    deep = P(both, None, None)
    return jax.shard_map(
        functools.partial(body, mesh.shape["grp"], mesh.shape["leaf"]),
        mesh=mesh,
        in_specs=(flat, flat, flat, flat, flat, deep, deep, P(), P(), P(), P()),
        out_specs=(flat, flat, flat),
        check_vma=False,
    )
```
